128 devices in a mesh: wide: 16 (over y, z), narrow: 8 (over x, core).
Axes of the slice: x: 4, y: 4, z: 4, core: 2. Of those that a mesh axis runs over, the one named last changes fastest.
Arguments:
- cold_table: float32 [131072, 512], P(('wide', 'narrow')), may hold values from -1.5 to 1.5
- cold_accum: float32 [131072], P(('wide', 'narrow')), may hold values from 0.01 to 1
- hot_table: float32 [2048, 512], replicated, may hold values from -1.5 to 1.5
- hot_accum: float32 [2048], replicated, may hold values from 0.01 to 1
- rel_table: float32 [2048, 512], replicated, may hold values from -3 to 3
- rel_accum: float32 [2048], replicated, may hold values from 0.01 to 1
- req_rows: int32 [128, 768], P(('wide', 'narrow')), may hold values from -1 to 1023, as said below
- head_slot: int32 [32768], P(('wide', 'narrow')), may hold values from 0 to 767, as said below
- tail_slot: int32 [32768], P(('wide', 'narrow')), may hold values from 0 to 767, as said below
- rel_ids: int32 [32768], P(('wide', 'narrow')), may hold values from 0 to 1023
- neg_ids: int32 [128, 1024], P(('wide', 'narrow')), may hold values from 0 to 2047
Outputs:
- new_cold: float32 [131072, 512], P(('wide', 'narrow'))
- new_cold_accum: float32 [131072], P(('wide', 'narrow'))
- new_hot: float32 [2048, 512], replicated
- new_hot_accum: float32 [2048], replicated
- new_rel: float32 [2048, 512], replicated
- new_rel_accum: float32 [2048], replicated
The draws below stay inside these ranges and needn't reach their ends.
Inputs may be any that keep to these rules, and one draw needn't show every extreme that they name: `req_rows`: in each block of 6 slots of one owner the used slots come first and name distinct rows of that owner; unused slots hold -1; every device uses all 6 slots of some owner. `head_slot`: always a used slot of req_rows of the same device; the owner is slot // 6. `tail_slot`: always a used slot of req_rows of the same device; the owner is slot // 6.
All inputs are finite; a program needn't handle non-finite values.
Results may differ from the reference program's by a relative error of at most 0.00075.
The reference program's roundings to bfloat16 on the way (of `p_low`) count: a program that leaves them out, or rounds other values in their place, can miss the bound.
Values may be sent and summed in bfloat16 or wider, within the bound.
A program may use at most 128 MiB of HBM per device.

```python
import math
import jax
import jax.numpy as jnp
from jax import lax

D = 512
REL = 1024
HOT = 2048
NEG = 1024
TRIP_DEV = 256
ROWS_DEV = 1024
CAP = 6
COLD = 131072
TRIPLES = 32768
DEVICES = 128


def request_plan(key):
    keys = jax.random.split(jax.random.fold_in(key, 11), 6)
    owners = jnp.arange(DEVICES, dtype=jnp.int32)
    favour = jax.random.randint(keys[0], (DEVICES,), 1, 5)
    level = jax.random.randint(keys[1], (DEVICES, DEVICES), 1, 5)
    counts = jnp.maximum(1, CAP * level * favour[None, :] // 16)
    full = jax.random.randint(keys[2], (DEVICES,), 0, DEVICES)
    full = full.at[0].set(DEVICES - 1)
    counts = jnp.where(owners[None, :] == full[:, None], CAP, counts)
    start = jax.random.randint(keys[3], (DEVICES, DEVICES, 1), 0, ROWS_DEV)
    place = jnp.arange(CAP, dtype=jnp.int32)
    rows = (start + place[None, None, :]) % ROWS_DEV
    rows = jnp.where(place[None, None, :] < counts[:, :, None], rows, -1).reshape(DEVICES, DEVICES * CAP)
    pick_owner = jax.random.randint(keys[4], (DEVICES, TRIP_DEV * 2), 0, DEVICES)
    live = jnp.take_along_axis(counts, pick_owner, axis=1)
    pick = jax.random.randint(keys[5], (DEVICES, TRIP_DEV * 2), 0, 1 << 20) % live
    slots = (pick_owner * CAP + pick).reshape(DEVICES, TRIP_DEV, 2)
    last_slot = DEVICES * CAP - 1
    slots = slots.at[0, 0, 0].set(last_slot).at[0, TRIP_DEV - 1, 1].set(last_slot)
    slots = slots.at[1, 0, 0].set(0).at[1, 0, 1].set(0)
    return (rows.astype(jnp.int32), slots.astype(jnp.int32))


def draw_req_rows(key, part):
    rows, slots = request_plan(key)
    return rows


def draw_head_slot(key, part):
    rows, slots = request_plan(key)
    return slots[:, :, 0].reshape(DEVICES * TRIP_DEV)


def draw_tail_slot(key, part):
    rows, slots = request_plan(key)
    return slots[:, :, 1].reshape(DEVICES * TRIP_DEV)


def draw_hot_table(key, part):
    inner = jax.random.fold_in(key, 3)
    base = 0.25 * jax.random.normal(inner, (HOT, D), jnp.float32)
    return jnp.clip(base, -1.5, 1.5)


def draw_cold_table(key, part):
    inner = jax.random.fold_in(key, 5)
    base = 0.25 * jax.random.normal(inner, (COLD, D), jnp.float32)
    return jnp.clip(base, -1.5, 1.5)


def draw_rel_table(key, part):
    inner = jax.random.fold_in(key, 7)
    base = jax.random.normal(inner, (2 * REL, D), jnp.float32)
    return jnp.clip(base, -3.0, 3.0)


def plant(entries, own_key, least, high):
    longest = entries.shape.index(max(entries.shape))
    spots = []
    for shift in (0, 1):
        where = [jax.random.randint(jax.random.fold_in(own_key, axis), (), 0, length) for axis, length in enumerate(entries.shape)]
        where[longest] = (where[longest] + shift) % entries.shape[longest]
        spots.append(tuple(where))
    return entries.at[spots[0]].set(least).at[spots[1]].set(high)


def block_levels(rng, dims, cuts, smallest, top_value):
    level = 1.0
    for position, parts in cuts:
        steps = jax.random.uniform(jax.random.fold_in(jax.random.fold_in(rng, 6), position), (parts,), jnp.float32, smallest / len(cuts), top_value / len(cuts))
        level = level * jnp.repeat(jnp.exp(steps), dims[position] // parts).reshape((-1,) + (1,) * (len(dims) - 1 - position))
    return level


def setup_inputs(seed: int = 0) -> dict:
    key_list = jax.random.split(jax.random.key(seed), 12)
    cold_table = draw_cold_table(jax.random.fold_in(key_list[11], 71), 0)
    cold_accum = jnp.clip(jnp.exp(math.log(1.0) - 4.6051702 * jax.random.uniform(key_list[1], (COLD,), jnp.float32) ** block_levels(key_list[1], (COLD,), ((0, 128),), -0.2, 0.2)), 0.01, 1.0)
    hot_table = draw_hot_table(jax.random.fold_in(key_list[11], 71), 0)
    hot_accum = jnp.clip(jnp.exp(jax.random.uniform(key_list[3], (HOT,), jnp.float32, math.log(0.01), math.log(1.0))), 0.01, 1.0)
    rel_table = draw_rel_table(jax.random.fold_in(key_list[11], 71), 0)
    rel_accum = jnp.clip(jnp.exp(jax.random.uniform(key_list[5], (2 * REL,), jnp.float32, math.log(0.01), math.log(1.0))), 0.01, 1.0)
    req_rows = draw_req_rows(jax.random.fold_in(key_list[11], 71), 0)
    head_slot = draw_head_slot(jax.random.fold_in(key_list[11], 71), 0)
    tail_slot = draw_tail_slot(jax.random.fold_in(key_list[11], 71), 0)
    rel_ids = plant(jax.random.randint(key_list[9], (TRIPLES,), 0, REL), jax.random.fold_in(key_list[9], 1), 0, REL - 1).astype(jnp.int32)
    neg_ids = plant(jax.random.randint(key_list[10], (DEVICES, NEG), 0, HOT), jax.random.fold_in(key_list[10], 1), 0, HOT - 1).astype(jnp.int32)
    return {"cold_table": cold_table, "cold_accum": cold_accum, "hot_table": hot_table, "hot_accum": hot_accum, "rel_table": rel_table, "rel_accum": rel_accum, "req_rows": req_rows, "head_slot": head_slot, "tail_slot": tail_slot, "rel_ids": rel_ids, "neg_ids": neg_ids}


def device_terms(head, tail, rel_fwd, rel_inv, negatives):
    queries = jnp.concatenate([head * rel_fwd, tail * rel_inv], axis=0)
    targets = jnp.concatenate([tail, head], axis=0)
    positive = lax.optimization_barrier(jnp.sum(queries * targets.astype(jnp.float32), axis=-1))
    query_low = queries.astype(jnp.bfloat16)
    scores = jnp.dot(query_low, negatives.T, preferred_element_type=jnp.float32)
    top = jnp.maximum(lax.optimization_barrier(jnp.max(scores, axis=-1)), positive)
    ex_neg = jnp.exp(scores - top[:, None])
    ex_pos = jnp.exp(positive - top)
    total = ex_pos + lax.optimization_barrier(jnp.sum(ex_neg, axis=-1))
    d_pos = ex_pos / total - 1.0
    p_low = (ex_neg / total[:, None]).astype(jnp.bfloat16)
    d_query = d_pos[:, None] * targets.astype(jnp.float32) + jnp.dot(p_low, negatives, preferred_element_type=jnp.float32)
    d_target = d_pos[:, None] * queries
    d_negatives = jnp.dot(p_low.T, query_low, preferred_element_type=jnp.float32)
    half = head.shape[0]
    d_head = d_query[:half] * rel_fwd + d_target[half:]
    d_tail = d_query[half:] * rel_inv + d_target[:half]
    d_fwd = d_query[:half] * head.astype(jnp.float32)
    d_inv = d_query[half:] * tail.astype(jnp.float32)
    return (d_head, d_tail, d_fwd, d_inv, d_negatives)

def adagrad(table, accum, grad):
    new_acc = accum + lax.optimization_barrier(jnp.mean(grad * grad, axis=-1))
    return (table - 0.1 * grad / jnp.sqrt(new_acc + 1e-06)[:, None], new_acc)

def reference(cold_table, cold_accum, hot_table, hot_accum, rel_table, rel_accum, req_rows, head_slot, tail_slot, rel_ids, neg_ids):
    heads = head_slot.reshape(DEVICES, TRIP_DEV)
    tails = tail_slot.reshape(DEVICES, TRIP_DEV)
    rels = rel_ids.reshape(DEVICES, TRIP_DEV)
    width = cold_table.shape[1]

    def step(carry, items):
        cold_g, hot_g, rel_g = carry
        dev, h_s, t_s, r_i, n_i = items
        row_map = req_rows[dev]
        h_id = h_s // CAP * ROWS_DEV + row_map[h_s]
        t_id = t_s // CAP * ROWS_DEV + row_map[t_s]
        head = cold_table[h_id].astype(jnp.bfloat16)
        tail = cold_table[t_id].astype(jnp.bfloat16)
        rel_fwd = rel_table[r_i]
        rel_inv = rel_table[r_i + REL]
        negatives = hot_table[n_i].astype(jnp.bfloat16)
        d_head, d_tail, d_fwd, d_inv, d_neg = device_terms(head, tail, rel_fwd, rel_inv, negatives)
        cold_g = cold_g.at[h_id].add(d_head).at[t_id].add(d_tail)
        hot_g = hot_g.at[n_i].add(d_neg)
        rel_g = rel_g.at[r_i].add(d_fwd).at[r_i + REL].add(d_inv)
        return ((cold_g, hot_g, rel_g), None)
    start = (jnp.zeros((COLD, width), jnp.float32), jnp.zeros((HOT, width), jnp.float32), jnp.zeros((2 * REL, width), jnp.float32))
    items = (jnp.arange(DEVICES, dtype=jnp.int32), heads, tails, rels, neg_ids)
    (cold_g, hot_g, rel_g), unused = lax.scan(step, start, items)
    new_cold, new_cold_accum = adagrad(cold_table, cold_accum, cold_g)
    new_hot, new_hot_accum = adagrad(hot_table, hot_accum, hot_g)
    new_rel, new_rel_accum = adagrad(rel_table, rel_accum, rel_g)
    return (new_cold, new_cold_accum, new_hot, new_hot_accum, new_rel, new_rel_accum)
```

```python
import functools
import jax
import jax.numpy as jnp
from jax import lax
from jax.experimental import pallas as pl
from jax.experimental.pallas import tpu as pltpu
from jax.sharding import PartitionSpec as P

REL = 1024
HOT = 2048
MESH = pl.DeviceIdType.MESH
F32 = jnp.float32
BF16 = jnp.bfloat16
ROT = ((0, 1, 2), (1, 2, 0), (2, 0, 1))
UNIT_ROT = (0, 0, 1, 2, 1, 1, 2, 2)
LANES = 128


def place():
    wide = lax.axis_index("wide")
    narrow = lax.axis_index("narrow")
    return (narrow // 2, wide // 4, wide % 4), narrow % 2


def device(coords, core):
    x, y, z = coords
    return (y * 4 + z, x * 2 + core)


def shifted(coords, axis, step):
    out = list(coords)
    out[axis] = (out[axis] + step) % 4
    return tuple(out)


def reduce_kernel(hot_ref, rel_ref, hot_out, rel_out, hot_pair, rel_pair, hot_sum, rel_sum, rel_low,
                  hot_r1, rel_r1, acc1, r2, acc2, r3, psend, precv, send, recv):
    coords, core = place()
    mate = device(coords, 1 - core)
    rows = HOT // 2

    barrier = pltpu.get_barrier_semaphore()
    pl.semaphore_signal(barrier, inc=1, device_id=mate, device_id_type=MESH)
    for axis in range(3):
        for step in (1, 2, 3):
            pl.semaphore_signal(barrier, inc=1, device_id=device(shifted(coords, axis, step), core), device_id_type=MESH)
    pl.semaphore_wait(barrier, 10)

    mine = pl.ds(pl.multiple_of(core * rows, rows), rows)
    other = pl.ds(pl.multiple_of((1 - core) * rows, rows), rows)
    pairs = []
    for k, (src, dst) in enumerate(((hot_ref, hot_pair), (rel_ref, rel_pair))):
        c = pltpu.make_async_remote_copy(src_ref=src.at[other], dst_ref=dst, send_sem=psend.at[k], recv_sem=precv.at[k],
                                         device_id=mate, device_id_type=MESH)
        c.start()
        pairs.append(c)

    def low(u):
        return u >= 4

    def cols(u):
        return slice((u % 4) * LANES, (u % 4 + 1) * LANES)

    def idx(u):
        r = ROT[UNIT_ROT[u]]
        return r, [coords[a] for a in r]

    def block(start, size):
        return pl.ds(pl.multiple_of(start, 16), size)

    copies = []

    def send_to(phase, u, axis, step, src, dst):
        c = pltpu.make_async_remote_copy(src_ref=src, dst_ref=dst, send_sem=send.at[phase, u, step - 1], recv_sem=recv.at[phase, u, step - 1],
                                         device_id=device(shifted(coords, axis, step), core), device_id_type=MESH)
        c.start()
        copies.append(c)
        return c

    phase1 = {}
    for k in range(2):
        pairs[k].wait_recv()
        if k == 0:
            hot_sum[...] = hot_ref[mine, :] + hot_pair[...]
        else:
            total = rel_ref[mine, :] + rel_pair[...]
            rel_sum[...] = total
            rel_low[...] = total.astype(BF16)
        for u in range(4 * k, 4 * k + 4):
            r, i = idx(u)
            src, dst = (rel_low, rel_r1.at[u - 4]) if low(u) else (hot_sum, hot_r1.at[u])
            for step in (1, 2, 3):
                j = (i[0] + step) % 4
                phase1[u, step] = send_to(0, u, r[0], step, src.at[block(j * 256, 256), cols(u)], dst.at[step - 1])
    phase2 = {}
    for u in range(8):
        r, i = idx(u)
        for step in (1, 2, 3):
            phase1[u, step].wait_recv()
        own = (rel_sum if low(u) else hot_sum)[block(i[0] * 256, 256), cols(u)]
        got = rel_r1[u - 4] if low(u) else hot_r1[u]
        acc1[u] = own + (got[0].astype(F32) + got[1].astype(F32) + got[2].astype(F32))
        for step in (1, 2, 3):
            j = (i[1] + step) % 4
            phase2[u, step] = send_to(1, u, r[1], step, acc1.at[u, block(j * 64, 64)], r2.at[u, step - 1])
    phase3 = {}
    for u in range(8):
        r, i = idx(u)
        for step in (1, 2, 3):
            phase2[u, step].wait_recv()
        acc2[u] = acc1[u, block(i[1] * 64, 64), :] + (r2[u, 0] + r2[u, 1] + r2[u, 2])
        for step in (1, 2, 3):
            j = (i[2] + step) % 4
            phase3[u, step] = send_to(2, u, r[2], step, acc2.at[u, block(j * 16, 16)], r3.at[u, step - 1])

    base = core * rows
    gathers = {}

    def gather(phase, u, level):
        r, i = idx(u)
        start = base
        size = 1024
        for a in range(level + 1):
            size //= 4
            start = start + i[a] * size
        out = rel_out if low(u) else hot_out
        ref = out.at[block(start, size), cols(u)]
        for step in (1, 2, 3):
            gathers[phase, u, step] = send_to(phase, u, r[level], step, ref, ref)

    for u in range(8):
        r, i = idx(u)
        for step in (1, 2, 3):
            phase3[u, step].wait_recv()
        total = acc2[u, block(i[2] * 16, 16), :] + (r3[u, 0] + r3[u, 1] + r3[u, 2])
        out = rel_out if low(u) else hot_out
        start = base + i[0] * 256 + i[1] * 64 + i[2] * 16
        out[block(start, 16), cols(u)] = total.astype(out.dtype)
        gather(3, u, 2)
    for level in (1, 0):
        for u in range(8):
            for step in (1, 2, 3):
                gathers[4 - level, u, step].wait_recv()
            gather(5 - level, u, level)
    last = []
    for u in range(8):
        for step in (1, 2, 3):
            gathers[5, u, step].wait_recv()
        out = rel_out if low(u) else hot_out
        ref = out.at[mine, cols(u)]
        c = pltpu.make_async_remote_copy(src_ref=ref, dst_ref=ref, send_sem=psend.at[2 + u], recv_sem=precv.at[2 + u],
                                         device_id=mate, device_id_type=MESH)
        c.start()
        last.append(c)
    for c in last:
        c.wait_recv()
    for c in pairs + copies + last:
        c.wait_send()


def all_sum(hot_grad, rel_grad):
    width = hot_grad.shape[1]
    vmem = pl.BlockSpec(memory_space=pltpu.VMEM)
    half = HOT // 2
    return pl.pallas_call(
        reduce_kernel,
        out_shape=(jax.ShapeDtypeStruct((HOT, width), F32), jax.ShapeDtypeStruct((2 * REL, width), BF16)),
        in_specs=[vmem, vmem],
        out_specs=(vmem, vmem),
        scratch_shapes=[
            pltpu.VMEM((half, width), F32), pltpu.VMEM((half, width), F32),
            pltpu.VMEM((half, width), F32), pltpu.VMEM((half, width), F32), pltpu.VMEM((half, width), BF16),
            pltpu.VMEM((4, 3, 256, LANES), F32), pltpu.VMEM((4, 3, 256, LANES), BF16),
            pltpu.VMEM((8, 256, LANES), F32), pltpu.VMEM((8, 3, 64, LANES), F32),
            pltpu.VMEM((8, 64, LANES), F32), pltpu.VMEM((8, 3, 16, LANES), F32),
            pltpu.SemaphoreType.DMA((10,)), pltpu.SemaphoreType.DMA((10,)),
            pltpu.SemaphoreType.DMA((6, 8, 3)), pltpu.SemaphoreType.DMA((6, 8, 3)),
        ],
        compiler_params=pltpu.CompilerParams(collective_id=0, has_side_effects=True, vmem_limit_bytes=60 << 20),
    )(hot_grad, rel_grad)


def device_terms(head, tail, rel_fwd, rel_inv, negatives):
    queries = jnp.concatenate([head * rel_fwd, tail * rel_inv], axis=0)
    targets = jnp.concatenate([tail, head], axis=0)
    positive = jnp.sum(queries * targets.astype(jnp.float32), axis=-1)
    query_low = queries.astype(jnp.bfloat16)
    scores = jnp.dot(query_low, negatives.T, preferred_element_type=jnp.float32)
    top = jnp.maximum(jnp.max(scores, axis=-1), positive)
    ex_neg = jnp.exp(scores - top[:, None])
    ex_pos = jnp.exp(positive - top)
    total = ex_pos + jnp.sum(ex_neg, axis=-1)
    d_pos = ex_pos / total - 1.0
    p_low = (ex_neg / total[:, None]).astype(jnp.bfloat16)
    d_query = d_pos[:, None] * targets.astype(jnp.float32) + jnp.dot(
        p_low, negatives, preferred_element_type=jnp.float32
    )
    d_target = d_pos[:, None] * queries
    d_negatives = jnp.dot(p_low.T, query_low, preferred_element_type=jnp.float32)
    half = head.shape[0]
    d_head = d_query[:half] * rel_fwd + d_target[half:]
    d_tail = d_query[half:] * rel_inv + d_target[:half]
    d_fwd = d_query[:half] * head.astype(jnp.float32)
    d_inv = d_query[half:] * tail.astype(jnp.float32)
    return (d_head, d_tail, d_fwd, d_inv, d_negatives)


def adagrad(table, accum, grad):
    new_acc = accum + jnp.mean(grad * grad, axis=-1)
    return (table - 0.1 * grad / jnp.sqrt(new_acc + 1e-06)[:, None], new_acc)


def on_device(
    cold_table,
    cold_accum,
    hot_table,
    hot_accum,
    rel_table,
    rel_accum,
    req_rows,
    head_slot,
    tail_slot,
    rel_ids,
    neg_ids,
):
    n_wide = lax.axis_size("wide")
    n_narrow = lax.axis_size("narrow")
    n_dev = n_wide * n_narrow
    rows_own, width = cold_table.shape
    slots_per = req_rows.shape[1] // n_dev
    wanted = req_rows.reshape(n_dev, slots_per)
    asked = lax.all_to_all(wanted, ("wide", "narrow"), split_axis=0, concat_axis=0, tiled=True)
    safe_rows = jnp.maximum(asked, 0).reshape(-1)
    served = cold_table[safe_rows].astype(jnp.bfloat16).reshape(n_dev, slots_per, width)
    fetched = lax.all_to_all(served, ("wide", "narrow"), split_axis=0, concat_axis=0, tiled=True)
    slot_rows = fetched.reshape(n_dev * slots_per, width)
    head = slot_rows[head_slot]
    tail = slot_rows[tail_slot]
    rel_fwd = rel_table[rel_ids]
    rel_inv = rel_table[rel_ids + REL]
    negatives = hot_table[neg_ids[0]].astype(jnp.bfloat16)
    d_head, d_tail, d_fwd, d_inv, d_neg = device_terms(head, tail, rel_fwd, rel_inv, negatives)
    slot_grad = jax.ops.segment_sum(
        jnp.concatenate([d_head, d_tail], axis=0),
        jnp.concatenate([head_slot, tail_slot]),
        num_segments=n_dev * slots_per,
    )
    rel_grad = jax.ops.segment_sum(
        jnp.concatenate([d_fwd, d_inv], axis=0),
        jnp.concatenate([rel_ids, rel_ids + REL]),
        num_segments=2 * REL,
    )
    hot_grad = jax.ops.segment_sum(d_neg, neg_ids[0], num_segments=HOT)
    outgoing = slot_grad.reshape(n_dev, slots_per, width)
    returned = lax.all_to_all(outgoing, ("wide", "narrow"), split_axis=0, concat_axis=0, tiled=True)
    cold_grad = jax.ops.segment_sum(returned.reshape(-1, width), safe_rows, num_segments=rows_own)
    new_cold, new_cold_accum = adagrad(cold_table, cold_accum, cold_grad)
    hot_sum, rel_sum = all_sum(hot_grad, rel_grad)
    new_hot, new_hot_accum = adagrad(hot_table, hot_accum, hot_sum)
    new_rel, new_rel_accum = adagrad(rel_table, rel_accum, rel_sum.astype(F32))
    return (new_cold, new_cold_accum, new_hot, new_hot_accum, new_rel, new_rel_accum)


def solution(mesh):
    in_specs = (
        P(("wide", "narrow"), None),
        P(("wide", "narrow")),
        P(),
        P(),
        P(),
        P(),
        P(("wide", "narrow"), None),
        P(("wide", "narrow")),
        P(("wide", "narrow")),
        P(("wide", "narrow")),
        P(("wide", "narrow"), None),
    )
    out_specs = (P(("wide", "narrow"), None), P(("wide", "narrow")), P(), P(), P(), P())
    return jax.shard_map(
        on_device, mesh=mesh, in_specs=in_specs, out_specs=out_specs, check_vma=False
    )
```
